128 devices in a mesh: orb: 32 (over z, x, core), grp: 4 (over y).
Axes of the slice: x: 4, y: 4, z: 4, core: 2. Of those that a mesh axis runs over, the one named last changes fastest.
Arguments:
- orbitals: float32 [1024, 32, 1024], P('orb', 'grp'), may hold values from -6 to 6
- anchors: int32 [1024], replicated, may hold values from 0 to 8
- wanted: int32 [32, 32, 1], replicated, may hold values from -1 to 1023, as said below
- pairs: int32 [32, 4, 240, 2], P('orb'), may hold values from 0 to 1023, as said below
- counts: int32 [32, 4], P('orb'), may hold values from 1 to 240, as said below
Outputs:
- exchange_field: float32 [1024, 32, 1024], P('orb', 'grp')
The draws below stay inside these ranges and needn't reach their ends.
Inputs may be any that keep to these rules, and one draw needn't show every extreme that they name: wanted[r, o] lists up to 1 different orbitals owned by group o (ids o * 32 to o * 32 + 31), -1 in empty slots; wanted[r, r] is empty; in every draw some pairs (r, o) fill all 1 slots. pairs[r, g, p] = (i, c) with i owned by group r and c below 64; a code below 32 never names i itself; pairs may repeat. `counts`: in each group r, one device g holds exactly 240 live pairs.
All inputs are finite; a program needn't handle non-finite values.
Results may differ from the reference program's by a relative error of at most 0.0085.
Values may be sent and summed in bfloat16 or wider, within the bound.
No kernel may reach another device: no remote copies, remote signals or barrier semaphores. Data moves between devices by JAX's collectives and lax.ppermute only.
A program may use at most 128 MiB of HBM per device.

```python
import math
import jax
import jax.numpy as jnp
from jax import lax

BOX = 32
SHIFT = 8
ORB_DEV = 32
CAP = 240
SLOT = 1
ORBITALS = 1024
N_ORB = 32
N_GRP = 4


def draw_orbitals(key, part):
    streams = jax.random.split(jax.random.fold_in(key, 37), 1)
    noise = jax.random.normal(streams[0], (ORBITALS, BOX, BOX * BOX), jnp.float32)
    values = noise
    return jnp.clip(values, -6.0, 6.0)


def make_lists(key):
    streams = jax.random.split(jax.random.fold_in(key, 29), 6)
    asking = jnp.arange(N_ORB, dtype=jnp.int32)[:, None, None]
    owning = jnp.arange(N_ORB, dtype=jnp.int32)[None, :, None]
    coin_flip = jax.random.randint(streams[0], (N_ORB, N_ORB, SLOT), 0, 2)
    forced = owning == (asking + 1) % N_ORB
    is_live = ((coin_flip == 1) | forced) & (owning != asking)
    scores = jax.random.randint(streams[1], (N_ORB, N_ORB, ORB_DEV), 0, 1 << 20) * ORB_DEV + jnp.arange(ORB_DEV, dtype=jnp.int32)
    chosen = jnp.argsort(scores, axis=-1)[..., :SLOT].astype(jnp.int32)
    wanted = jnp.where(is_live, owning * ORB_DEV + chosen, -1).astype(jnp.int32)
    flat_rows = wanted.reshape(N_ORB, N_ORB * SLOT)
    alive = (flat_rows >= 0).astype(jnp.int32)
    number = jnp.sum(alive, axis=1)
    ordinal = jnp.cumsum(alive, axis=1) - 1
    extent = (N_ORB, N_GRP, CAP)
    group_ids = jnp.arange(N_ORB, dtype=jnp.int32)[:, None, None]
    first_local = jax.random.randint(streams[2], extent, 0, ORB_DEV)
    stride = jax.random.randint(streams[3], extent, 1, ORB_DEV)
    own_code = (first_local + stride) % ORB_DEV
    picked = jax.random.randint(streams[4], extent, 0, 1 << 20) % number[:, None, None]
    matches = (ordinal[:, None, None, :] == picked[..., None]) & (alive[:, None, None, :] == 1)
    positions = jnp.arange(N_ORB * SLOT, dtype=jnp.int32)
    far_code = ORB_DEV + jnp.sum(jnp.where(matches, positions, 0), axis=-1)
    side_flip = jax.random.randint(streams[5], extent, 0, 2)
    second_code = jnp.where(side_flip == 0, own_code, far_code)
    first_ids = group_ids * ORB_DEV + first_local
    pairs = jnp.stack([first_ids, second_code], axis=-1).astype(jnp.int32)
    return (wanted, pairs)


def draw_wanted(key, part):
    return make_lists(key)[0]


def draw_pairs(key, part):
    return make_lists(key)[1]


def draw_counts(key, part):
    streams = jax.random.split(jax.random.fold_in(key, 31), 2)
    heaviest = jax.random.randint(streams[0], (N_ORB, 1), 0, N_GRP)
    lighter = jax.random.randint(streams[1], (N_ORB, N_GRP), max(1, CAP // 8), CAP // 3 + 1)
    return jnp.where(jnp.arange(N_GRP, dtype=jnp.int32)[None, :] == heaviest, CAP, lighter).astype(jnp.int32)


def plant(result, own_key, low, top_value):
    shape = result.shape
    index_at = [jax.random.randint(jax.random.fold_in(own_key, axis), (), 0, shape[axis]) for axis in range(len(shape))]
    result = result.at[tuple(index_at)].set(low)
    longest = shape.index(max(shape))
    index_at[longest] = (index_at[longest] + 1) % shape[longest]
    return result.at[tuple(index_at)].set(top_value)


def setup_inputs(seed: int = 0) -> dict:
    key_of = jax.random.split(jax.random.key(seed), 6)
    return {
        "orbitals": draw_orbitals(jax.random.fold_in(key_of[5], 71), 0),
        "anchors": plant(jax.random.randint(key_of[1], (ORBITALS,), 0, SHIFT + 1), jax.random.fold_in(key_of[1], 1), 0, SHIFT).astype(jnp.int32),
        "wanted": draw_wanted(jax.random.fold_in(key_of[5], 71), 0),
        "pairs": draw_pairs(jax.random.fold_in(key_of[5], 71), 0),
        "counts": draw_counts(jax.random.fold_in(key_of[5], 71), 0),
    }


screening = 0.01
block_pairs = 16

def sine_table(extent):
    ordinal = jnp.arange(extent, dtype=jnp.float32) + 1.0
    angles = math.pi * ordinal[:, None] * ordinal[None, :] / (extent + 1)
    return (math.sqrt(2.0 / (extent + 1)) * jnp.sin(angles)).astype(jnp.bfloat16)

def denominator(extent):
    ordinal = jnp.arange(extent, dtype=jnp.float32) + 1.0
    eigenvalue = 4.0 * jnp.sin(math.pi * ordinal / (2 * (extent + 1))) ** 2
    return eigenvalue[:, None, None] + eigenvalue[None, :, None] + eigenvalue[None, None, :] + screening

def displaced(box_batch, offset):
    margin = box_batch.shape[1] // 4
    padded = jnp.pad(box_batch, ((0, 0), (margin, margin), (0, 0)))

    def single(source, start_row):
        return lax.dynamic_slice_in_dim(source, start_row, box_batch.shape[1], 0)
    return jax.vmap(single)(padded, (margin - offset).astype(jnp.int32))

def potential(density, sine_rows, divisor):
    sine_wide = sine_rows.astype(jnp.float32)

    def along(values, form):
        return jnp.einsum(form, sine_wide, values.astype(jnp.float32), precision=lax.Precision.HIGHEST)
    section_one = along(density, 'kx,pxyz->pkyz').astype(jnp.bfloat16)
    section_two = along(section_one, 'kz,pxyz->pxyk').astype(jnp.bfloat16)
    section_three = (along(section_two, 'ky,pxyz->pxkz') / divisor).astype(jnp.bfloat16)
    section_four = along(section_three, 'ky,pxyz->pxkz').astype(jnp.bfloat16)
    section_five = along(section_four, 'kz,pxyz->pxyk').astype(jnp.bfloat16)
    return along(section_five, 'kx,pxyz->pkyz').astype(jnp.bfloat16)

def pair_terms(first_boxes, second_boxes, offset, sine_rows, divisor):
    batch_size, extent, plane_size = first_boxes.shape
    shifted_box = displaced(second_boxes, offset)
    density = (first_boxes.astype(jnp.float32) * shifted_box.astype(jnp.float32)).astype(jnp.bfloat16)
    field_cube = potential(density.reshape(batch_size, extent, extent, extent), sine_rows, divisor)
    field_wide = field_cube.reshape(batch_size, extent, plane_size).astype(jnp.float32)
    own_term = field_wide * shifted_box.astype(jnp.float32)
    other_term = displaced(field_wide * first_boxes.astype(jnp.float32), -offset)
    return (own_term, other_term)

def reference(orbitals, anchors, wanted, pairs, counts):
    orbit_count, extent, plane_size = orbitals.shape
    group_total, group_size, capacity = (pairs.shape[0], pairs.shape[1], pairs.shape[2])
    own_count = orbit_count // group_total
    request_flat = wanted.reshape(group_total, -1).astype(jnp.int32)
    request_width = request_flat.shape[1]
    group_row = jnp.broadcast_to(jnp.arange(group_total, dtype=jnp.int32)[:, None, None], (group_total, group_size, capacity)).reshape(-1)
    raw_pairs = pairs.reshape(-1, 2).astype(jnp.int32)
    code = raw_pairs[:, 1]
    far_index = jnp.clip(code - own_count, 0, request_width - 1).astype(jnp.int32)
    far_id = request_flat[group_row, far_index]
    second_full = jnp.where(code < own_count, group_row * own_count + code, far_id).astype(jnp.int32)
    flat_pairs = jnp.stack([raw_pairs[:, 0], second_full], axis=-1).astype(jnp.int32)
    slot_total = flat_pairs.shape[0]
    is_live = (jnp.arange(capacity, dtype=jnp.int32)[None, None, :] < counts[:, :, None]).reshape(-1)
    is_live = is_live & (second_full >= 0)
    ranking = (jnp.cumsum(is_live.astype(jnp.int32)) - 1).astype(jnp.int32)
    live_total = jnp.sum(is_live.astype(jnp.int32))
    target = jnp.where(is_live, ranking, slot_total + block_pairs).astype(jnp.int32)
    listed = jnp.zeros((slot_total + block_pairs, 2), jnp.int32).at[target].set(flat_pairs, mode='drop')
    boxes = orbitals.astype(jnp.bfloat16)
    sine_rows = sine_table(extent)
    divisor = denominator(extent)

    def turn(turn_index, running):
        start_row = (turn_index * block_pairs).astype(jnp.int32)
        window = lax.dynamic_slice_in_dim(listed, start_row, block_pairs, 0)
        first_ids = window[:, 0]
        second_ids = window[:, 1]
        in_range = start_row + jnp.arange(block_pairs, dtype=jnp.int32) < live_total
        offset = (anchors[second_ids] - anchors[first_ids]).astype(jnp.int32)
        own_term, other_term = pair_terms(boxes[first_ids], boxes[second_ids], offset, sine_rows, divisor)
        running = running.at[jnp.where(in_range, first_ids, orbit_count)].add(own_term, mode='drop')
        running = running.at[jnp.where(in_range, second_ids, orbit_count)].add(other_term, mode='drop')
        return running
    rounds = (live_total + block_pairs - 1) // block_pairs
    initial = jnp.zeros((orbit_count, extent, plane_size), jnp.float32)
    return lax.fori_loop(0, rounds, turn, initial)
```

```python
import math

import jax
import jax.numpy as jnp
import numpy as np
from jax import lax
from jax.experimental import pallas as pl
from jax.experimental.pallas import tpu as pltpu
from jax.sharding import PartitionSpec as P

screening = 0.01
EXT = 32
HALF = EXT // 2
PLANE = EXT * EXT
CHUNKS = PLANE // 128
MARGIN = 8
PAD = EXT + 2 * MARGIN
BATCH = 8
LIST = 256
F32 = jnp.float32
BF16 = jnp.bfloat16


def tables():
    ordinal = np.arange(EXT, dtype=np.float64) + 1.0
    sine = math.sqrt(2.0 / (EXT + 1)) * np.sin(math.pi * ordinal[:, None] * ordinal[None, :] / (EXT + 1))
    sine = sine.astype(np.float32).astype(jnp.bfloat16).astype(np.float64)
    eigen = 4.0 * np.sin(math.pi * ordinal / (2 * (EXT + 1))) ** 2
    blocks, inverse = [], []
    for y_odd in (0, 1):
        for z_odd in (0, 1):
            blocks.append(np.kron(sine[:HALF, y_odd::2], sine[:HALF, z_odd::2]))
            plane = (eigen[y_odd::2, None] + eigen[None, z_odd::2]).reshape(-1)
            inverse.append(1.0 / (eigen[:, None] + plane[None, :] + screening))
    return (
        np.stack(blocks).astype(jnp.bfloat16),
        np.kron(np.eye(BATCH), sine).astype(jnp.bfloat16),
        np.stack(inverse).astype(np.float32),
    )


def source_of(position):
    quadrant = position >> 8
    y = (position >> 4) & 15
    z = position & 15
    y = jnp.where((quadrant & 2) != 0, EXT - 1 - y, y)
    z = jnp.where((quadrant & 1) != 0, EXT - 1 - z, z)
    return y * EXT + z


def order_kernel(wanted, orbitals, slab, outgoing, matrix, ordered):
    member = lax.axis_index("orb")
    for c in range(CHUNKS):
        source = source_of(lax.broadcasted_iota(jnp.int32, (PLANE, 128), 1) + c * 128)
        row = lax.broadcasted_iota(jnp.int32, (PLANE, 128), 0)
        matrix[:, c * 128 : (c + 1) * 128] = (row == source).astype(F32).astype(BF16)
    ordered[...] = jnp.dot(orbitals[...].astype(BF16), matrix[...], preferred_element_type=F32)
    slab[...] = ordered[...].astype(BF16)

    def local(r):
        return jnp.clip(wanted[r, member] - member * 32, 0, 31)

    for r in range(0, 32, 2):
        low = ordered[pl.ds(pl.multiple_of(local(r) * 8, 8), 8), :]
        high = ordered[pl.ds(pl.multiple_of(local(r + 1) * 8, 8), 8), :]
        outgoing[r * 8 : r * 8 + 16, :] = jnp.concatenate([low, high], axis=0).astype(BF16)


def list_kernel(pairs, counts, wanted, anchors, own_list, far_list, totals, table):
    member = lax.axis_index("orb")
    position = lax.axis_index("grp")

    def clear(k, carry):
        for u in range(16):
            table[k * 16 + u] = 0
        return carry

    lax.fori_loop(0, 32 * 64 // 16, clear, 0)

    def blank(k, carry):
        for u in range(8):
            own_list[k * 8 + u] = MARGIN << 11
            far_list[k * 8 + u] = MARGIN << 11
        return carry

    lax.fori_loop(0, LIST // 8, blank, 0)
    for g in range(4):

        def note(p, carry):
            cell = (pairs[g, p * 2] & 31) * 64 + pairs[g, p * 2 + 1]
            table[cell] = table[cell] + 1
            return carry

        lax.fori_loop(0, counts[0, g], note, 0)

    def collect(first, target):
        def one(k, found):
            i = k >> 5
            c = (k & 31) + first
            weight = table[i * 64 + c]
            if first:
                other = wanted[member, c - 32]
            else:
                other = member * 32 + c
            live = (weight > 0) & (other >= 0)

            @pl.when(live & ((found & 3) == position))
            def _():
                d = anchors[jnp.maximum(other, 0)] - anchors[member * 32 + i]
                target[found >> 2] = i | (c << 5) | ((d + MARGIN) << 11) | (weight << 16)

            return found + live.astype(jnp.int32)

        found = lax.fori_loop(0, 32 * 32, one, 0)
        return (found - position + 3) >> 2

    totals[0] = collect(0, own_list)
    totals[1] = collect(32, far_list)


def unpack_slab(block, rows, boxes, base, member_of):
    start = pl.multiple_of(MARGIN + 8 * member_of, 8)

    def one(k, carry):
        for c in range(CHUNKS):
            part = block[pl.ds(k * 16, 16), c * 128 : (c + 1) * 128].astype(F32)
            boxes[pl.ds(base + 2 * k, 2), c, pl.ds(start, 8), :] = part.reshape(2, 8, 128)
        return carry

    lax.fori_loop(0, rows // 16, one, 0)


def fill(refs, boxes, base):
    position = lax.axis_index("grp")
    own, left, right, far_low, far_high = refs
    unpack_slab(own, 256, boxes, base, position)
    unpack_slab(left, 256, boxes, base, (position + 3) & 3)
    unpack_slab(right, 256, boxes, base, (position + 1) & 3)
    unpack_slab(far_low, 128, boxes, base, (position + 2) & 3)
    unpack_slab(far_high, 128, boxes, base + 16, (position + 2) & 3)


def run_pairs(count, listed, boxes, sums, blocks, along_x, inverse, density, field):
    def fields(entry):
        return (entry & 31, (entry >> 5) & 63, MARGIN + MARGIN - ((entry >> 11) & 31), entry >> 16)

    def batch(b, carry):
        for p in range(BATCH):
            i, j, shifted, weight = fields(listed[b * BATCH + p])
            for h in range(2):
                f = []
                for q in range(4):
                    c = 2 * q + h
                    f.append(boxes[i, c, pl.ds(MARGIN, EXT), :] * boxes[j, c, pl.ds(shifted, EXT), :])
                a, bb, cc, d = f
                s1, s2, s3, s4 = a + bb, a - bb, cc + d, cc - d
                for q, v in enumerate((s1 + s3, s2 + s4, s1 - s3, s2 - s4)):
                    density[q, p * EXT : (p + 1) * EXT, h * 128 : (h + 1) * 128] = v.astype(BF16)
        for q in range(4):
            t = jnp.dot(density[q], blocks[q], preferred_element_type=F32).astype(BF16)
            t = jnp.dot(along_x[...], t, preferred_element_type=F32)
            t = (t.reshape(BATCH, EXT, 256) * inverse[q][None]).reshape(BATCH * EXT, 256).astype(BF16)
            t = jnp.dot(along_x[...], t, preferred_element_type=F32).astype(BF16)
            field[q] = lax.dot_general(t, blocks[q], (((1,), (1,)), ((), ())), preferred_element_type=F32)
        for p in range(BATCH):
            i, j, shifted, weight = fields(listed[b * BATCH + p])
            scale = weight.astype(F32)
            for h in range(2):
                ee, eo, oe, oo = (
                    field[q, p * EXT : (p + 1) * EXT, h * 128 : (h + 1) * 128] for q in range(4)
                )
                s1, s2, s3, s4 = ee + eo, ee - eo, oe + oo, oe - oo
                for q, v in enumerate((s1 + s3, s2 + s4, s1 - s3, s2 - s4)):
                    c = 2 * q + h
                    v = v * scale
                    sums[i, c, pl.ds(MARGIN, EXT), :] += v * boxes[j, c, pl.ds(shifted, EXT), :]
                    sums[j, c, pl.ds(shifted, EXT), :] += v * boxes[i, c, pl.ds(MARGIN, EXT), :]
        return carry

    lax.fori_loop(0, (count + BATCH - 1) // BATCH, batch, 0)


def clear_rows(ref, first, last):
    def one(k, carry):
        ref[pl.ds(first + k, 1)] = jnp.zeros((1,) + ref.shape[1:], F32)
        return carry

    lax.fori_loop(0, last - first, one, 0)


def own_kernel(totals, listed, s, r, l, r2, l2, blocks, along_x, inverse, out, boxes, sums, density, field):
    clear_rows(boxes, 0, 32)
    clear_rows(sums, 0, 32)
    fill((s, r, l, r2, l2), boxes, 0)
    run_pairs(totals[0], listed, boxes, sums, blocks, along_x, inverse, density, field)

    def one(k, carry):
        for c in range(CHUNKS):
            out[pl.ds(k, 1), c] = sums[pl.ds(k, 1), c, MARGIN : MARGIN + EXT, :]
        return carry

    lax.fori_loop(0, 32, one, 0)


def pack_sums(sums, base, outs):
    position = lax.axis_index("grp")
    for step in range(4):
        start = pl.multiple_of(MARGIN + 8 * ((position + step) & 3), 8)

        def one(k, carry):
            for c in range(CHUNKS):
                part = sums[pl.ds(base + 2 * k, 2), c, pl.ds(start, 8), :].reshape(16, 128)
                outs[step][pl.ds(k * 16, 16), c * 128 : (c + 1) * 128] = part.astype(BF16)
            return carry

        lax.fori_loop(0, 16, one, 0)


def far_kernel(
    totals, listed, before,
    s, r, l, r2, l2,
    fs, fr, fl, fr2, fl2,
    blocks, along_x, inverse,
    o0, o1, o2, o3, f0, f1, f2, f3,
    boxes, sums, density, field,
):
    clear_rows(boxes, 0, 64)
    clear_rows(sums, 32, 64)
    fill((s, r, l, r2, l2), boxes, 0)
    fill((fs, fr, fl, fr2, fl2), boxes, 32)

    def one(k, carry):
        for c in range(CHUNKS):
            sums[pl.ds(k, 1), c, MARGIN : MARGIN + EXT, :] = before[pl.ds(k, 1), c]
        return carry

    lax.fori_loop(0, 32, one, 0)
    run_pairs(totals[1], listed, boxes, sums, blocks, along_x, inverse, density, field)
    pack_sums(sums, 0, (o0, o1, o2, o3))
    pack_sums(sums, 32, (f0, f1, f2, f3))


def finish_kernel(wanted, p0, p1, p2, p3, returned, out, matrix, total):
    member = lax.axis_index("orb")
    for c in range(CHUNKS):
        source = source_of(lax.broadcasted_iota(jnp.int32, (PLANE, 128), 0))
        column = lax.broadcasted_iota(jnp.int32, (PLANE, 128), 1) + c * 128
        matrix[:, c * 128 : (c + 1) * 128] = (column == source).astype(F32).astype(BF16)
    total[...] = (p0[...].astype(F32) + p1[...].astype(F32)) + (p2[...].astype(F32) + p3[...].astype(F32))
    for r in range(0, 32, 2):
        both = returned[r * 8 : r * 8 + 16, :].astype(F32)
        for u in range(2):
            asked = wanted[r + u, member]
            row = pl.multiple_of(jnp.clip(asked - member * 32, 0, 31) * 8, 8)

            @pl.when(asked >= 0)
            def _():
                total[pl.ds(row, 8), :] += both[u * 8 : (u + 1) * 8]

    value = total[...]
    high = value.astype(BF16)
    low = (value - high.astype(F32)).astype(BF16)
    out[...] = jnp.dot(high, matrix[...], preferred_element_type=F32) + jnp.dot(
        low, matrix[...], preferred_element_type=F32
    )


SMEM = pl.BlockSpec(memory_space=pltpu.SMEM)
VMEM = pl.BlockSpec(memory_space=pltpu.VMEM)


def call(kernel, name, ins, outs, scratch):
    return pl.pallas_call(
        kernel,
        name=name,
        in_specs=ins,
        out_specs=[spec for spec, _ in outs],
        out_shape=[shape for _, shape in outs],
        scratch_shapes=scratch,
        compiler_params=pltpu.CompilerParams(vmem_limit_bytes=60 << 20),
    )


def ring(slab):
    up = [(k, (k + 1) % 4) for k in range(4)]
    down = [(k, (k + 3) % 4) for k in range(4)]
    left = lax.ppermute(slab, "grp", up)
    right = lax.ppermute(slab, "grp", down)
    far_low = lax.ppermute(left[:128], "grp", up)
    far_high = lax.ppermute(right[128:], "grp", down)
    return (slab, left, right, far_low, far_high)


def scatter(parts):
    got = [parts[0]]
    for k in (1, 2, 3):
        got.append(lax.ppermute(parts[k], "grp", [(m, (m + k) % 4) for m in range(4)]))
    return got


def shards(orbitals, anchors, wanted, pairs, counts):
    blocks, along_x, inverse = (jnp.asarray(t) for t in tables())
    wanted = wanted.reshape(32, 32)
    slab_type = jax.ShapeDtypeStruct((256, PLANE), BF16)
    slab, outgoing = call(
        order_kernel, "order", [SMEM, VMEM], [(VMEM, slab_type)] * 2,
        [pltpu.VMEM((PLANE, PLANE), BF16), pltpu.VMEM((256, PLANE), F32)],
    )(wanted, orbitals.reshape(256, PLANE))
    own = ring(slab)
    incoming = lax.all_to_all(outgoing, "orb", split_axis=0, concat_axis=0, tiled=True)
    list_type = jax.ShapeDtypeStruct((LIST,), jnp.int32)
    own_list, far_list, totals = call(
        list_kernel, "lists", [SMEM] * 4,
        [(SMEM, list_type), (SMEM, list_type), (SMEM, jax.ShapeDtypeStruct((2,), jnp.int32))],
        [pltpu.SMEM((32 * 64,), jnp.int32)],
    )(pairs.reshape(4, -1), counts, wanted, anchors)
    far = ring(incoming)

    def work(total):
        return [
            pltpu.VMEM((total, CHUNKS, PAD, 128), F32),
            pltpu.VMEM((total, CHUNKS, PAD, 128), F32),
            pltpu.VMEM((4, BATCH * EXT, 256), BF16),
            pltpu.VMEM((4, BATCH * EXT, 256), F32),
        ]

    (before,) = call(
        own_kernel, "own", [SMEM] * 2 + [VMEM] * 8,
        [(VMEM, jax.ShapeDtypeStruct((32, CHUNKS, EXT, 128), F32))], work(32),
    )(totals, own_list, *own, blocks, along_x, inverse)
    parts = call(
        far_kernel, "far", [SMEM] * 2 + [VMEM] * 14, [(VMEM, slab_type)] * 8, work(64),
    )(totals, far_list, before, *own, *far, blocks, along_x, inverse)
    far_got = scatter(parts[4:])
    own_got = scatter(parts[:4])
    far_sum = sum(part.astype(F32) for part in far_got).astype(BF16)
    returned = lax.all_to_all(far_sum, "orb", split_axis=0, concat_axis=0, tiled=True)
    (result,) = call(
        finish_kernel, "finish", [SMEM] + [VMEM] * 5,
        [(VMEM, jax.ShapeDtypeStruct((256, PLANE), F32))],
        [pltpu.VMEM((PLANE, PLANE), BF16), pltpu.VMEM((256, PLANE), F32)],
    )(wanted, *own_got, returned)
    return result.reshape(32, 8, PLANE)


def solution(mesh):
    return jax.shard_map(
        shards,
        mesh=mesh,
        in_specs=(P("orb", "grp", None), P(), P(), P("orb", None, None, None), P("orb", None)),
        out_specs=P("orb", "grp", None),
        check_vma=False,
    )
```

```python
import math

import jax
import jax.numpy as jnp
import numpy as np
from jax import lax
from jax.experimental import pallas as pl
from jax.experimental.pallas import tpu as pltpu
from jax.sharding import PartitionSpec as P

screening = 0.01
EXT = 32
HALF = EXT // 2
PLANE = EXT * EXT
CHUNKS = PLANE // 128
MARGIN = 8
PAD = EXT + 2 * MARGIN
BATCH = 8
LIST = 256
F32 = jnp.float32
BF16 = jnp.bfloat16


def tables():
    ordinal = np.arange(EXT, dtype=np.float64) + 1.0
    sine = math.sqrt(2.0 / (EXT + 1)) * np.sin(math.pi * ordinal[:, None] * ordinal[None, :] / (EXT + 1))
    sine = sine.astype(np.float32).astype(jnp.bfloat16).astype(np.float64)
    eigen = 4.0 * np.sin(math.pi * ordinal / (2 * (EXT + 1))) ** 2
    blocks, inverse = [], []
    for y_odd in (0, 1):
        for z_odd in (0, 1):
            blocks.append(np.kron(sine[:HALF, y_odd::2], sine[:HALF, z_odd::2]))
            plane = (eigen[y_odd::2, None] + eigen[None, z_odd::2]).reshape(-1)
            inverse.append(1.0 / (eigen[:, None] + plane[None, :] + screening))
    return (
        np.stack(blocks).astype(jnp.bfloat16),
        np.kron(np.eye(BATCH), sine).astype(jnp.bfloat16),
        np.stack(inverse).astype(np.float32),
    )


def source_of(position):
    quadrant = position >> 8
    y = (position >> 4) & 15
    z = position & 15
    y = jnp.where((quadrant & 2) != 0, EXT - 1 - y, y)
    z = jnp.where((quadrant & 1) != 0, EXT - 1 - z, z)
    return y * EXT + z


def order_kernel(wanted, orbitals, slab, outgoing, matrix, ordered):
    member = lax.axis_index("orb")
    for c in range(CHUNKS):
        source = source_of(lax.broadcasted_iota(jnp.int32, (PLANE, 128), 1) + c * 128)
        row = lax.broadcasted_iota(jnp.int32, (PLANE, 128), 0)
        matrix[:, c * 128 : (c + 1) * 128] = (row == source).astype(F32).astype(BF16)
    ordered[...] = jnp.dot(orbitals[...].astype(BF16), matrix[...], preferred_element_type=F32)
    slab[...] = ordered[...].astype(BF16)

    def local(r):
        return jnp.clip(wanted[r, member] - member * 32, 0, 31)

    for r in range(0, 32, 2):
        low = ordered[pl.ds(pl.multiple_of(local(r) * 8, 8), 8), :]
        high = ordered[pl.ds(pl.multiple_of(local(r + 1) * 8, 8), 8), :]
        outgoing[r * 8 : r * 8 + 16, :] = jnp.concatenate([low, high], axis=0).astype(BF16)


def list_kernel(counts, pairs, wanted, own_list, far_list):
    member = lax.axis_index("orb")
    position = lax.axis_index("grp")
    weights = jnp.zeros((64, 32), F32)
    slot = lax.broadcasted_iota(jnp.int32, (1, 240), 1)
    for g in range(4):
        live = slot < counts[0, g]
        first = jnp.where(live, pairs[g, 0:1, :] & 31, -1)
        code = jnp.where(live, pairs[g, 1:2, :], -1)
        first_hot = (lax.broadcasted_iota(jnp.int32, (32, 240), 0) == first).astype(F32).astype(BF16)
        code_hot = (lax.broadcasted_iota(jnp.int32, (64, 240), 0) == code).astype(F32).astype(BF16)
        weights += lax.dot_general(code_hot, first_hot, (((1,), (1,)), ((), ())), preferred_element_type=F32)
    down = lax.broadcasted_iota(jnp.int32, (32, 32), 0)
    across = lax.broadcasted_iota(jnp.int32, (32, 32), 1)
    asked = jnp.where(down == across, wanted[pl.ds(member, 1), :], 0)
    asked = jnp.sum(asked.astype(F32), axis=1, keepdims=True) >= 0.0
    lower = (across <= down).astype(F32).astype(BF16)
    before = (down < across).astype(F32).astype(BF16)
    lane = lax.broadcasted_iota(jnp.int32, (1, LIST), 1)
    for half, target in ((0, own_list), (1, far_list)):
        weight = weights[half * 32 : half * 32 + 32]
        live = weight > 0.5
        if half:
            live = live & asked
        mask = live.astype(F32)
        inner = jnp.dot(lower, mask.astype(BF16), preferred_element_type=F32)
        total = jnp.broadcast_to(inner[31:32], (8, 32))
        outer = jnp.dot(total.astype(BF16), before, preferred_element_type=F32)[0:1]
        rank = (outer + inner).astype(jnp.int32) - 1
        key = jnp.where(live & ((rank & 3) == position), rank >> 2, -1)
        entry = across | (down << 5) | (weight.astype(jnp.int32) << 11)
        found = jnp.zeros((32, LIST), jnp.int32)
        for i in range(32):
            found += jnp.where(key[:, i : i + 1] == lane, entry[:, i : i + 1], 0)
        packed = jnp.sum(found, axis=0, keepdims=True)
        every = jnp.sum(total[0:1], axis=1, keepdims=True).astype(jnp.int32)
        target[...] = jnp.where(lane == LIST - 1, (every - position + 3) >> 2, packed)


def make_lists(counts, pairs, wanted):
    list_type = jax.ShapeDtypeStruct((1, LIST), jnp.int32)
    return call(
        list_kernel, "lists", [SMEM, VMEM, VMEM], [(VMEM, list_type)] * 2, [],
    )(counts, jnp.transpose(pairs[0], (0, 2, 1)), wanted)


def unpack_slab(block, rows, boxes, base, member_of):
    start = pl.multiple_of(MARGIN + 8 * member_of, 8)

    def one(k, carry):
        for c in range(CHUNKS):
            part = block[pl.ds(k * 16, 16), c * 128 : (c + 1) * 128].astype(F32)
            boxes[pl.ds(base + 2 * k, 2), c, pl.ds(start, 8), :] = part.reshape(2, 8, 128)
        return carry

    lax.fori_loop(0, rows // 16, one, 0)


def fill(refs, boxes, base):
    position = lax.axis_index("grp")
    own, left, right, far_low, far_high = refs
    unpack_slab(own, 256, boxes, base, position)
    unpack_slab(left, 256, boxes, base, (position + 3) & 3)
    unpack_slab(right, 256, boxes, base, (position + 1) & 3)
    unpack_slab(far_low, 128, boxes, base, (position + 2) & 3)
    unpack_slab(far_high, 128, boxes, base + 16, (position + 2) & 3)


def run_pairs(base, anchors, wanted, listed, boxes, sums, blocks, along_x, inverse, density, field):
    member = lax.axis_index("orb")
    count = listed[0, LIST - 1]

    def fields(entry):
        i = entry & 31
        c = (entry >> 5) & 31
        if base:
            other = jnp.maximum(wanted[member, c], 0)
        else:
            other = member * 32 + c
        shifted = MARGIN + anchors[member * 32 + i] - anchors[other]
        return (i, base + c, shifted, entry >> 11)

    def batch(b, carry):
        for p in range(BATCH):
            i, j, shifted, weight = fields(listed[0, b * BATCH + p])
            for h in range(2):
                f = []
                for q in range(4):
                    c = 2 * q + h
                    f.append(boxes[i, c, pl.ds(MARGIN, EXT), :] * boxes[j, c, pl.ds(shifted, EXT), :])
                a, bb, cc, d = f
                s1, s2, s3, s4 = a + bb, a - bb, cc + d, cc - d
                for q, v in enumerate((s1 + s3, s2 + s4, s1 - s3, s2 - s4)):
                    density[q, p * EXT : (p + 1) * EXT, h * 128 : (h + 1) * 128] = v.astype(BF16)
        for q in range(4):
            t = jnp.dot(density[q], blocks[q], preferred_element_type=F32).astype(BF16)
            t = jnp.dot(along_x[...], t, preferred_element_type=F32)
            t = (t.reshape(BATCH, EXT, 256) * inverse[q][None]).reshape(BATCH * EXT, 256).astype(BF16)
            t = jnp.dot(along_x[...], t, preferred_element_type=F32).astype(BF16)
            field[q] = lax.dot_general(t, blocks[q], (((1,), (1,)), ((), ())), preferred_element_type=F32)
        for p in range(BATCH):
            i, j, shifted, weight = fields(listed[0, b * BATCH + p])
            scale = weight.astype(F32)
            for h in range(2):
                ee, eo, oe, oo = (
                    field[q, p * EXT : (p + 1) * EXT, h * 128 : (h + 1) * 128] for q in range(4)
                )
                s1, s2, s3, s4 = ee + eo, ee - eo, oe + oo, oe - oo
                for q, v in enumerate((s1 + s3, s2 + s4, s1 - s3, s2 - s4)):
                    c = 2 * q + h
                    v = v * scale
                    sums[i, c, pl.ds(MARGIN, EXT), :] += v * boxes[j, c, pl.ds(shifted, EXT), :]
                    sums[j, c, pl.ds(shifted, EXT), :] += v * boxes[i, c, pl.ds(MARGIN, EXT), :]
        return carry

    lax.fori_loop(0, (count + BATCH - 1) // BATCH, batch, 0)


def clear_rows(ref, first, last):
    def one(k, carry):
        ref[pl.ds(first + k, 1)] = jnp.zeros((1,) + ref.shape[1:], F32)
        return carry

    lax.fori_loop(0, last - first, one, 0)


def own_kernel(anchors, wanted, listed, s, r, l, r2, l2, blocks, along_x, inverse, out, boxes, sums, density, field):
    clear_rows(boxes, 0, 32)
    clear_rows(sums, 0, 32)
    fill((s, r, l, r2, l2), boxes, 0)
    run_pairs(0, anchors, wanted, listed, boxes, sums, blocks, along_x, inverse, density, field)

    def one(k, carry):
        for c in range(CHUNKS):
            out[pl.ds(k, 1), c] = sums[pl.ds(k, 1), c, MARGIN : MARGIN + EXT, :]
        return carry

    lax.fori_loop(0, 32, one, 0)


def pack_sums(sums, base, outs):
    position = lax.axis_index("grp")
    own, ahead, low, high, behind = outs
    for step, first, target in ((2, 0, low), (2, 16, high), (1, 0, ahead), (3, 0, behind), (0, 0, own)):
        start = pl.multiple_of(MARGIN + 8 * ((position + step) & 3), 8)

        def one(k, carry):
            for c in range(CHUNKS):
                part = sums[pl.ds(base + first + 2 * k, 2), c, pl.ds(start, 8), :].reshape(16, 128)
                target[pl.ds(k * 16, 16), c * 128 : (c + 1) * 128] = part.astype(BF16)
            return carry

        lax.fori_loop(0, target.shape[0] // 16, one, 0)


def far_kernel(
    anchors, wanted, listed, before,
    s, r, l, r2, l2,
    fs, fr, fl, fr2, fl2,
    blocks, along_x, inverse,
    o0, o1, o2, o3, o4, f0, f1, f2, f3, f4,
    boxes, sums, density, field,
):
    clear_rows(boxes, 0, 64)
    clear_rows(sums, 32, 64)
    fill((s, r, l, r2, l2), boxes, 0)
    fill((fs, fr, fl, fr2, fl2), boxes, 32)

    def one(k, carry):
        for c in range(CHUNKS):
            sums[pl.ds(k, 1), c, MARGIN : MARGIN + EXT, :] = before[pl.ds(k, 1), c]
        return carry

    lax.fori_loop(0, 32, one, 0)
    run_pairs(32, anchors, wanted, listed, boxes, sums, blocks, along_x, inverse, density, field)
    pack_sums(sums, 32, (f0, f1, f2, f3, f4))
    pack_sums(sums, 0, (o0, o1, o2, o3, o4))


def finish_kernel(wanted, p0, p1, p2, returned, out, matrix, total):
    member = lax.axis_index("orb")
    for c in range(CHUNKS):
        source = source_of(lax.broadcasted_iota(jnp.int32, (PLANE, 128), 0))
        column = lax.broadcasted_iota(jnp.int32, (PLANE, 128), 1) + c * 128
        matrix[:, c * 128 : (c + 1) * 128] = (column == source).astype(F32).astype(BF16)
    total[...] = p0[...].astype(F32) + p1[...].astype(F32) + p2[...].astype(F32)
    for r in range(0, 32, 2):
        both = returned[r * 8 : r * 8 + 16, :].astype(F32)
        for u in range(2):
            asked = wanted[r + u, member]
            row = pl.multiple_of(jnp.clip(asked - member * 32, 0, 31) * 8, 8)

            @pl.when(asked >= 0)
            def _():
                total[pl.ds(row, 8), :] += both[u * 8 : (u + 1) * 8]

    value = total[...]
    high = value.astype(BF16)
    low = (value - high.astype(F32)).astype(BF16)
    out[...] = jnp.dot(high, matrix[...], preferred_element_type=F32) + jnp.dot(
        low, matrix[...], preferred_element_type=F32
    )


SMEM = pl.BlockSpec(memory_space=pltpu.SMEM)
VMEM = pl.BlockSpec(memory_space=pltpu.VMEM)


def call(kernel, name, ins, outs, scratch):
    return pl.pallas_call(
        kernel,
        name=name,
        in_specs=ins,
        out_specs=[spec for spec, _ in outs],
        out_shape=[shape for _, shape in outs],
        scratch_shapes=scratch,
        compiler_params=pltpu.CompilerParams(vmem_limit_bytes=60 << 20),
    )


def ring(slab):
    up = [(k, (k + 1) % 4) for k in range(4)]
    down = [(k, (k + 3) % 4) for k in range(4)]
    left = lax.ppermute(slab, "grp", up)
    right = lax.ppermute(slab, "grp", down)
    far_low = lax.ppermute(left[:128], "grp", up)
    far_high = lax.ppermute(right[128:], "grp", down)
    return (slab, left, right, far_low, far_high)


def scatter(parts):
    up = [(k, (k + 1) % 4) for k in range(4)]
    down = [(k, (k + 3) % 4) for k in range(4)]
    own, ahead, low, high, behind = parts
    low = lax.ppermute(low, "grp", up)
    high = lax.ppermute(high, "grp", down)

    def add(a, b):
        return (a.astype(F32) + b.astype(F32)).astype(BF16)

    ahead = jnp.concatenate([add(ahead[:128], low), ahead[128:]], axis=0)
    behind = jnp.concatenate([behind[:128], add(behind[128:], high)], axis=0)
    return (own, lax.ppermute(ahead, "grp", up), lax.ppermute(behind, "grp", down))


def shards(orbitals, anchors, wanted, pairs, counts):
    blocks, along_x, inverse = (jnp.asarray(t) for t in tables())
    wanted = wanted.reshape(32, 32)
    slab_type = jax.ShapeDtypeStruct((256, PLANE), BF16)
    slab, outgoing = call(
        order_kernel, "order", [SMEM, VMEM], [(VMEM, slab_type)] * 2,
        [pltpu.VMEM((PLANE, PLANE), BF16), pltpu.VMEM((256, PLANE), F32)],
    )(wanted, orbitals.reshape(256, PLANE))
    own = ring(slab)
    incoming = lax.all_to_all(outgoing, "orb", split_axis=0, concat_axis=0, tiled=True)
    own_list, far_list = make_lists(counts, pairs, wanted)
    far = ring(incoming)

    def work(total):
        return [
            pltpu.VMEM((total, CHUNKS, PAD, 128), F32),
            pltpu.VMEM((total, CHUNKS, PAD, 128), F32),
            pltpu.VMEM((4, BATCH * EXT, 256), BF16),
            pltpu.VMEM((4, BATCH * EXT, 256), F32),
        ]

    (before,) = call(
        own_kernel, "own", [SMEM] * 3 + [VMEM] * 8,
        [(VMEM, jax.ShapeDtypeStruct((32, CHUNKS, EXT, 128), F32))], work(32),
    )(anchors, wanted, own_list, *own, blocks, along_x, inverse)
    half_type = jax.ShapeDtypeStruct((128, PLANE), BF16)
    packed = [(VMEM, t) for t in (slab_type, slab_type, half_type, half_type, slab_type)]
    parts = call(
        far_kernel, "far", [SMEM] * 3 + [VMEM] * 14, packed * 2, work(64),
    )(anchors, wanted, far_list, before, *own, *far, blocks, along_x, inverse)
    far_got = scatter(parts[5:])
    own_got = scatter(parts[:5])
    far_sum = sum(part.astype(F32) for part in far_got).astype(BF16)
    returned = lax.all_to_all(far_sum, "orb", split_axis=0, concat_axis=0, tiled=True)
    (result,) = call(
        finish_kernel, "finish", [SMEM] + [VMEM] * 4,
        [(VMEM, jax.ShapeDtypeStruct((256, PLANE), F32))],
        [pltpu.VMEM((PLANE, PLANE), BF16), pltpu.VMEM((256, PLANE), F32)],
    )(wanted, *own_got, returned)
    return result.reshape(32, 8, PLANE)


def solution(mesh):
    return jax.shard_map(
        shards,
        mesh=mesh,
        in_specs=(P("orb", "grp", None), P(), P(), P("orb", None, None, None), P("orb", None)),
        out_specs=P("orb", "grp", None),
        check_vma=False,
    )
```

```python
import math

import jax
import jax.numpy as jnp
import numpy as np
from jax import lax
from jax.experimental import pallas as pl
from jax.experimental.pallas import tpu as pltpu
from jax.sharding import PartitionSpec as P

screening = 0.01
EXT = 32
HALF = EXT // 2
PLANE = EXT * EXT
CHUNKS = PLANE // 128
MARGIN = 8
PAD = EXT + 2 * MARGIN
BATCH = 8
LIST = 256
F32 = jnp.float32
BF16 = jnp.bfloat16


def tables():
    ordinal = np.arange(EXT, dtype=np.float64) + 1.0
    sine = math.sqrt(2.0 / (EXT + 1)) * np.sin(math.pi * ordinal[:, None] * ordinal[None, :] / (EXT + 1))
    sine = sine.astype(np.float32).astype(jnp.bfloat16).astype(np.float64)
    eigen = 4.0 * np.sin(math.pi * ordinal / (2 * (EXT + 1))) ** 2
    blocks, inverse = [], []
    for y_odd in (0, 1):
        for z_odd in (0, 1):
            blocks.append(np.kron(sine[:HALF, y_odd::2], sine[:HALF, z_odd::2]))
            plane = (eigen[y_odd::2, None] + eigen[None, z_odd::2]).reshape(-1)
            inverse.append(1.0 / (eigen[:, None] + plane[None, :] + screening))
    return (
        np.stack(blocks).astype(jnp.bfloat16),
        np.kron(np.eye(BATCH), sine).astype(jnp.bfloat16),
        np.stack(inverse).astype(np.float32),
    )


def source_of(position):
    quadrant = position >> 8
    y = (position >> 4) & 15
    z = position & 15
    y = jnp.where((quadrant & 2) != 0, EXT - 1 - y, y)
    z = jnp.where((quadrant & 1) != 0, EXT - 1 - z, z)
    return y * EXT + z


def order_kernel(wanted, orbitals, slab, outgoing, matrix, ordered):
    member = lax.axis_index("orb")
    for c in range(CHUNKS):
        source = source_of(lax.broadcasted_iota(jnp.int32, (PLANE, 128), 1) + c * 128)
        row = lax.broadcasted_iota(jnp.int32, (PLANE, 128), 0)
        matrix[:, c * 128 : (c + 1) * 128] = (row == source).astype(F32).astype(BF16)
    ordered[...] = jnp.dot(orbitals[...].astype(BF16), matrix[...], preferred_element_type=F32)
    slab[...] = ordered[...].astype(BF16)

    def local(r):
        return jnp.clip(wanted[r, member] - member * 32, 0, 31)

    for r in range(0, 32, 2):
        low = ordered[pl.ds(pl.multiple_of(local(r) * 8, 8), 8), :]
        high = ordered[pl.ds(pl.multiple_of(local(r + 1) * 8, 8), 8), :]
        outgoing[r * 8 : r * 8 + 16, :] = jnp.concatenate([low, high], axis=0).astype(BF16)


def list_kernel(counts, pairs, wanted, own_list, far_list):
    member = lax.axis_index("orb")
    position = lax.axis_index("grp")
    weights = jnp.zeros((64, 32), F32)
    slot = lax.broadcasted_iota(jnp.int32, (1, 240), 1)
    for g in range(4):
        live = slot < counts[0, g]
        first = jnp.where(live, pairs[g, 0:1, :] & 31, -1)
        code = jnp.where(live, pairs[g, 1:2, :], -1)
        first_hot = (lax.broadcasted_iota(jnp.int32, (32, 240), 0) == first).astype(F32).astype(BF16)
        code_hot = (lax.broadcasted_iota(jnp.int32, (64, 240), 0) == code).astype(F32).astype(BF16)
        weights += lax.dot_general(code_hot, first_hot, (((1,), (1,)), ((), ())), preferred_element_type=F32)
    down = lax.broadcasted_iota(jnp.int32, (32, 32), 0)
    across = lax.broadcasted_iota(jnp.int32, (32, 32), 1)
    asked = jnp.where(down == across, wanted[pl.ds(member, 1), :], 0)
    asked = jnp.sum(asked.astype(F32), axis=1, keepdims=True) >= 0.0
    lower = (across <= down).astype(F32).astype(BF16)
    before = (down < across).astype(F32).astype(BF16)
    lane = lax.broadcasted_iota(jnp.int32, (1, LIST), 1)
    for half, target in ((0, own_list), (1, far_list)):
        weight = weights[half * 32 : half * 32 + 32]
        live = weight > 0.5
        if half:
            live = live & asked
        mask = live.astype(F32)
        inner = jnp.dot(lower, mask.astype(BF16), preferred_element_type=F32)
        total = jnp.broadcast_to(inner[31:32], (8, 32))
        outer = jnp.dot(total.astype(BF16), before, preferred_element_type=F32)[0:1]
        rank = (outer + inner).astype(jnp.int32) - 1
        key = jnp.where(live & ((rank & 3) == position), rank >> 2, -1)
        entry = across | (down << 5) | (weight.astype(jnp.int32) << 11)
        found = jnp.zeros((32, LIST), jnp.int32)
        for i in range(32):
            found += jnp.where(key[:, i : i + 1] == lane, entry[:, i : i + 1], 0)
        packed = jnp.sum(found, axis=0, keepdims=True)
        every = jnp.sum(total[0:1], axis=1, keepdims=True).astype(jnp.int32)
        target[...] = jnp.where(lane == LIST - 1, (every - position + 3) >> 2, packed)


def make_lists(counts, pairs, wanted):
    list_type = jax.ShapeDtypeStruct((1, LIST), jnp.int32)
    return call(
        list_kernel, "lists", [SMEM, VMEM, VMEM], [(VMEM, list_type)] * 2, [],
    )(counts, jnp.transpose(pairs[0], (0, 2, 1)), wanted)


def unpack_slab(block, rows, boxes, base, member_of):
    start = pl.multiple_of(MARGIN + 8 * member_of, 8)

    def one(k, carry):
        for c in range(CHUNKS):
            part = block[pl.ds(k * 16, 16), c * 128 : (c + 1) * 128].astype(F32)
            boxes[pl.ds(base + 2 * k, 2), c, pl.ds(start, 8), :] = part.reshape(2, 8, 128)
        return carry

    lax.fori_loop(0, rows // 16, one, 0)


def fill(refs, boxes, base):
    position = lax.axis_index("grp")
    own, left, right, far_low, far_high = refs
    unpack_slab(own, 256, boxes, base, position)
    unpack_slab(left, 256, boxes, base, (position + 3) & 3)
    unpack_slab(right, 256, boxes, base, (position + 1) & 3)
    unpack_slab(far_low, 128, boxes, base, (position + 2) & 3)
    unpack_slab(far_high, 128, boxes, base + 16, (position + 2) & 3)


def run_pairs(base, anchors, wanted, listed, boxes, sums, blocks, along_x, inverse, work):
    density, one, two, three, field = work
    first, second = sums
    member = lax.axis_index("orb")
    batches = (listed[0, LIST - 1] + BATCH - 1) // BATCH
    field[...] = jnp.zeros_like(field)

    def fields(k):
        entry = listed[0, k]
        i = entry & 31
        c = (entry >> 5) & 31
        if base:
            other = jnp.maximum(wanted[member, c], 0)
        else:
            other = member * 32 + c
        shifted = MARGIN + anchors[member * 32 + i] - anchors[other]
        return (i, c, shifted, (entry >> 11).astype(F32))

    def part(p, h):
        return (slice(p * EXT, (p + 1) * EXT), slice(h * 128, (h + 1) * 128))

    def quads(a, b, c, d):
        s1, s2, s3, s4 = a + b, a - b, c + d, c - d
        return (s1 + s3, s2 + s4, s1 - s3, s2 - s4)

    def product(b, p):
        i, c, shifted, _ = fields(b * BATCH + p)
        for h in range(2):
            f = [
                boxes[i, 2 * q + h, pl.ds(MARGIN, EXT), :] * boxes[base + c, 2 * q + h, pl.ds(shifted, EXT), :]
                for q in range(4)
            ]
            rows, lanes = part(p, h)
            for q, v in enumerate(quads(*f)):
                density[q, rows, lanes] = v.astype(BF16)

    def terms(b, p):
        i, c, shifted, weight = fields(b * BATCH + p)
        for h in range(2):
            rows, lanes = part(p, h)
            v = [u * weight for u in quads(*(field[q, rows, lanes] for q in range(4)))]
            for q in range(4):
                first[i, 2 * q + h] += v[q] * boxes[base + c, 2 * q + h, pl.ds(shifted, EXT), :]
            for q in range(4):
                second[c, 2 * q + h, pl.ds(shifted, EXT), :] += v[q] * boxes[i, 2 * q + h, pl.ds(MARGIN, EXT), :]

    def step(stage, q):
        if stage == 0:
            one[q] = jnp.dot(density[q], blocks[q], preferred_element_type=F32).astype(BF16)
        elif stage == 1:
            t = jnp.dot(along_x[...], one[q], preferred_element_type=F32)
            two[q] = (t.reshape(BATCH, EXT, 256) * inverse[q][None]).reshape(BATCH * EXT, 256).astype(BF16)
        elif stage == 2:
            three[q] = jnp.dot(along_x[...], two[q], preferred_element_type=F32).astype(BF16)
        else:
            field[q] = lax.dot_general(three[q], blocks[q], (((1,), (1,)), ((), ())), preferred_element_type=F32)

    def batch(b, carry):
        for k in range(8):
            step(k // 4, k % 4)
            terms(jnp.maximum(b - 1, 0), k)
        for k in range(8):
            step(2 + k // 4, k % 4)
            product(b + 1, k)
        return carry

    for p in range(BATCH):
        product(0, p)
    lax.fori_loop(0, batches, batch, 0)
    for p in range(BATCH):
        terms(jnp.maximum(batches - 1, 0), p)


def prepare(boxes, sums):
    first, second = sums

    def margins(k, carry):
        for c in range(CHUNKS):
            boxes[k, c, 0:MARGIN, :] = jnp.zeros((MARGIN, 128), F32)
            boxes[k, c, MARGIN + EXT : PAD, :] = jnp.zeros((MARGIN, 128), F32)
        return carry

    lax.fori_loop(0, boxes.shape[0], margins, 0)

    def blank(k, carry):
        first[pl.ds(k, 1)] = jnp.zeros((1, CHUNKS, EXT, 128), F32)
        second[pl.ds(k, 1)] = jnp.zeros((1, CHUNKS, PAD, 128), F32)
        return carry

    lax.fori_loop(0, 32, blank, 0)


def pack_sums(outs, terms):
    position = lax.axis_index("grp")
    own, ahead, low, high, behind = range(5)
    for step, first, target in ((2, 0, low), (2, 16, high), (1, 0, ahead), (3, 0, behind), (0, 0, own)):
        start = 8 * ((position + step) & 3)

        def one(k, carry):
            for c in range(CHUNKS):
                value = None
                for ref, margin in terms:
                    rows = pl.ds(pl.multiple_of(start + margin, 8), 8)
                    term = ref[pl.ds(first + 2 * k, 2), c, rows, :].reshape(16, 128)
                    value = term if value is None else value + term
                outs[target][pl.ds(pl.multiple_of(k * 16, 16), 16), c * 128 : (c + 1) * 128] = value.astype(BF16)
            return carry

        lax.fori_loop(0, outs[target].shape[0] // 16, one, 0)


def unpack_sums(ins, ref):
    position = lax.axis_index("grp")
    own, ahead, low, high, behind = ins
    for step, first, source in ((2, 0, low), (2, 16, high), (1, 0, ahead), (3, 0, behind), (0, 0, own)):
        start = pl.multiple_of(8 * ((position + step) & 3), 8)

        def one(k, carry):
            for c in range(CHUNKS):
                part = source[pl.ds(pl.multiple_of(k * 16, 16), 16), c * 128 : (c + 1) * 128].astype(F32)
                ref[pl.ds(first + 2 * k, 2), c, pl.ds(start, 8), :] = part.reshape(2, 8, 128)
            return carry

        lax.fori_loop(0, source.shape[0] // 16, one, 0)


def own_kernel(anchors, wanted, listed, s, r, l, r2, l2, blocks, along_x, inverse, *rest):
    outs, boxes, sums, work = rest[:5], rest[5], rest[6:8], rest[8:]
    prepare(boxes, sums)
    fill((s, r, l, r2, l2), boxes, 0)
    run_pairs(0, anchors, wanted, listed, boxes, sums, blocks, along_x, inverse, work)
    pack_sums(outs, ((sums[0], 0), (sums[1], MARGIN)))


def far_kernel(anchors, wanted, listed, *rest):
    before, own, far = rest[:5], rest[5:10], rest[10:15]
    blocks, along_x, inverse = rest[15:18]
    own_outs, far_outs, boxes, sums, work = rest[18:23], rest[23:28], rest[28], rest[29:31], rest[31:]
    prepare(boxes, sums)
    fill(own, boxes, 0)
    fill(far, boxes, 32)
    unpack_sums(before, sums[0])
    run_pairs(32, anchors, wanted, listed, boxes, sums, blocks, along_x, inverse, work)
    pack_sums(far_outs, ((sums[1], MARGIN),))
    pack_sums(own_outs, ((sums[0], 0),))


def scratch(total):
    stage = pltpu.VMEM((4, BATCH * EXT, 256), BF16)
    return [
        pltpu.VMEM((total, CHUNKS, PAD, 128), F32),
        pltpu.VMEM((32, CHUNKS, EXT, 128), F32),
        pltpu.VMEM((32, CHUNKS, PAD, 128), F32),
        stage, stage, stage, stage,
        pltpu.VMEM((4, BATCH * EXT, 256), F32),
    ]


def finish_kernel(wanted, p0, p1, p2, returned, out, matrix, total):
    member = lax.axis_index("orb")
    for c in range(CHUNKS):
        source = source_of(lax.broadcasted_iota(jnp.int32, (PLANE, 128), 0))
        column = lax.broadcasted_iota(jnp.int32, (PLANE, 128), 1) + c * 128
        matrix[:, c * 128 : (c + 1) * 128] = (column == source).astype(F32).astype(BF16)
    total[...] = p0[...].astype(F32) + p1[...].astype(F32) + p2[...].astype(F32)
    for r in range(0, 32, 2):
        both = returned[r * 8 : r * 8 + 16, :].astype(F32)
        for u in range(2):
            asked = wanted[r + u, member]
            row = pl.multiple_of(jnp.clip(asked - member * 32, 0, 31) * 8, 8)

            @pl.when(asked >= 0)
            def _():
                total[pl.ds(row, 8), :] += both[u * 8 : (u + 1) * 8]

    value = total[...]
    high = value.astype(BF16)
    low = (value - high.astype(F32)).astype(BF16)
    out[...] = jnp.dot(high, matrix[...], preferred_element_type=F32) + jnp.dot(
        low, matrix[...], preferred_element_type=F32
    )


SMEM = pl.BlockSpec(memory_space=pltpu.SMEM)
VMEM = pl.BlockSpec(memory_space=pltpu.VMEM)


SLAB = jax.ShapeDtypeStruct((256, PLANE), BF16)
HALF_SLAB = jax.ShapeDtypeStruct((128, PLANE), BF16)
PARTS = [(VMEM, shape) for shape in (SLAB, SLAB, HALF_SLAB, HALF_SLAB, SLAB)]


def call(kernel, name, ins, outs, scratch):
    return pl.pallas_call(
        kernel,
        name=name,
        in_specs=ins,
        out_specs=[spec for spec, _ in outs],
        out_shape=[shape for _, shape in outs],
        scratch_shapes=scratch,
        compiler_params=pltpu.CompilerParams(vmem_limit_bytes=60 << 20),
    )


def ring(slab):
    up = [(k, (k + 1) % 4) for k in range(4)]
    down = [(k, (k + 3) % 4) for k in range(4)]
    left = lax.ppermute(slab, "grp", up)
    right = lax.ppermute(slab, "grp", down)
    far_low = lax.ppermute(left[:128], "grp", up)
    far_high = lax.ppermute(right[128:], "grp", down)
    return (slab, left, right, far_low, far_high)


def scatter(parts):
    up = [(k, (k + 1) % 4) for k in range(4)]
    down = [(k, (k + 3) % 4) for k in range(4)]
    own, ahead, low, high, behind = parts
    low = lax.ppermute(low, "grp", up)
    high = lax.ppermute(high, "grp", down)

    def add(a, b):
        return (a.astype(F32) + b.astype(F32)).astype(BF16)

    ahead = jnp.concatenate([add(ahead[:128], low), ahead[128:]], axis=0)
    behind = jnp.concatenate([behind[:128], add(behind[128:], high)], axis=0)
    return (own, lax.ppermute(ahead, "grp", up), lax.ppermute(behind, "grp", down))


def shards(orbitals, anchors, wanted, pairs, counts):
    blocks, along_x, inverse = (jnp.asarray(t) for t in tables())
    wanted = wanted.reshape(32, 32)
    slab, outgoing = call(
        order_kernel, "order", [SMEM, VMEM], [(VMEM, SLAB)] * 2,
        [pltpu.VMEM((PLANE, PLANE), BF16), pltpu.VMEM((256, PLANE), F32)],
    )(wanted, orbitals.reshape(256, PLANE))
    own = ring(slab)
    incoming = lax.all_to_all(outgoing, "orb", split_axis=0, concat_axis=0, tiled=True)
    own_list, far_list = make_lists(counts, pairs, wanted)
    far = ring(incoming)

    tables_in = (blocks, along_x, inverse)
    before = call(own_kernel, "own", [SMEM] * 3 + [VMEM] * 8, PARTS, scratch(32))(
        anchors, wanted, own_list, *own, *tables_in
    )
    parts = call(far_kernel, "far", [SMEM] * 3 + [VMEM] * 18, PARTS * 2, scratch(64))(
        anchors, wanted, far_list, *before, *own, *far, *tables_in
    )
    far_got = scatter(parts[5:])
    own_got = scatter(parts[:5])
    far_sum = sum(part.astype(F32) for part in far_got).astype(BF16)
    returned = lax.all_to_all(far_sum, "orb", split_axis=0, concat_axis=0, tiled=True)
    (result,) = call(
        finish_kernel, "finish", [SMEM] + [VMEM] * 4,
        [(VMEM, jax.ShapeDtypeStruct((256, PLANE), F32))],
        [pltpu.VMEM((PLANE, PLANE), BF16), pltpu.VMEM((256, PLANE), F32)],
    )(wanted, *own_got, returned)
    return result.reshape(32, 8, PLANE)


def solution(mesh):
    return jax.shard_map(
        shards,
        mesh=mesh,
        in_specs=(P("orb", "grp", None), P(), P(), P("orb", None, None, None), P("orb", None)),
        out_specs=P("orb", "grp", None),
        check_vma=False,
    )
```

```python
import functools
import math

import jax
import jax.numpy as jnp
import numpy as np
from jax import lax
from jax.experimental import pallas as pl
from jax.experimental.pallas import tpu as pltpu
from jax.sharding import PartitionSpec as P


screening = 0.01
EXT = 32
HALF = EXT // 2
PLANE = EXT * EXT
CHUNKS = PLANE // 128
MARGIN = 8
PAD = EXT + 2 * MARGIN
BATCH = 8
LIST = 256
F32 = jnp.float32
BF16 = jnp.bfloat16


def tables():
    ordinal = np.arange(EXT, dtype=np.float64) + 1.0
    sine = math.sqrt(2.0 / (EXT + 1)) * np.sin(math.pi * ordinal[:, None] * ordinal[None, :] / (EXT + 1))
    sine = sine.astype(np.float32).astype(jnp.bfloat16).astype(np.float64)
    eigen = 4.0 * np.sin(math.pi * ordinal / (2 * (EXT + 1))) ** 2
    blocks, inverse = [], []
    for y_odd in (0, 1):
        for z_odd in (0, 1):
            blocks.append(np.kron(sine[:HALF, y_odd::2], sine[:HALF, z_odd::2]))
            plane = (eigen[y_odd::2, None] + eigen[None, z_odd::2]).reshape(-1)
            inverse.append(1.0 / (eigen[:, None] + plane[None, :] + screening))
    return (
        np.stack(blocks).astype(jnp.bfloat16),
        np.kron(np.eye(BATCH), sine).astype(jnp.bfloat16),
        np.stack(inverse).astype(np.float32),
    )


def source_of(position):
    quadrant = position >> 8
    y = (position >> 4) & 15
    z = position & 15
    y = jnp.where((quadrant & 2) != 0, EXT - 1 - y, y)
    z = jnp.where((quadrant & 1) != 0, EXT - 1 - z, z)
    return y * EXT + z


def order_kernel(wanted, orbitals, slab, outgoing, matrix, ordered):
    member = lax.axis_index("orb")
    for c in range(CHUNKS):
        source = source_of(lax.broadcasted_iota(jnp.int32, (PLANE, 128), 1) + c * 128)
        row = lax.broadcasted_iota(jnp.int32, (PLANE, 128), 0)
        matrix[:, c * 128 : (c + 1) * 128] = (row == source).astype(F32).astype(BF16)
    ordered[...] = jnp.dot(orbitals[...].astype(BF16), matrix[...], preferred_element_type=F32)
    slab[...] = ordered[...].astype(BF16)

    def local(r):
        return jnp.clip(wanted[r, member] - member * 32, 0, 31)

    for r in range(0, 32, 2):
        low = ordered[pl.ds(pl.multiple_of(local(r) * 8, 8), 8), :]
        high = ordered[pl.ds(pl.multiple_of(local(r + 1) * 8, 8), 8), :]
        outgoing[r * 8 : r * 8 + 16, :] = jnp.concatenate([low, high], axis=0).astype(BF16)


def list_kernel(counts, pairs, wanted, own_list, low_list, high_list):
    member = lax.axis_index("orb")
    position = lax.axis_index("grp")
    weights = jnp.zeros((64, 32), F32)
    slot = lax.broadcasted_iota(jnp.int32, (1, 240), 1)
    for g in range(4):
        live = slot < counts[0, g]
        first = jnp.where(live, pairs[g, 0:1, :] & 31, -1)
        code = jnp.where(live, pairs[g, 1:2, :], -1)
        first_hot = (lax.broadcasted_iota(jnp.int32, (32, 240), 0) == first).astype(F32).astype(BF16)
        code_hot = (lax.broadcasted_iota(jnp.int32, (64, 240), 0) == code).astype(F32).astype(BF16)
        weights += lax.dot_general(code_hot, first_hot, (((1,), (1,)), ((), ())), preferred_element_type=F32)
    down = lax.broadcasted_iota(jnp.int32, (32, 32), 0)
    across = lax.broadcasted_iota(jnp.int32, (32, 32), 1)
    asked = jnp.where(down == across, wanted[pl.ds(member, 1), :], 0)
    asked = jnp.sum(asked.astype(F32), axis=1, keepdims=True) >= 0.0
    lower = (across <= down).astype(F32).astype(BF16)
    before = (down < across).astype(F32).astype(BF16)
    lane = lax.broadcasted_iota(jnp.int32, (1, LIST), 1)
    for half, target in ((0, own_list), (1, low_list), (2, high_list)):
        weight = weights[32 if half else 0 : 64 if half else 32]
        live = weight > 0.5
        if half:
            live = live & asked & ((down >> 4) == half - 1)
        mask = live.astype(F32)
        inner = jnp.dot(lower, mask.astype(BF16), preferred_element_type=F32)
        total = jnp.broadcast_to(inner[31:32], (8, 32))
        outer = jnp.dot(total.astype(BF16), before, preferred_element_type=F32)[0:1]
        rank = (outer + inner).astype(jnp.int32) - 1
        key = jnp.where(live & ((rank & 3) == position), rank >> 2, -1)
        entry = across | ((down & 15 if half else down) << 5) | (weight.astype(jnp.int32) << 11)
        found = jnp.zeros((32, LIST), jnp.int32)
        for i in range(32):
            found += jnp.where(key[:, i : i + 1] == lane, entry[:, i : i + 1], 0)
        packed = jnp.sum(found, axis=0, keepdims=True)
        every = jnp.sum(total[0:1], axis=1, keepdims=True).astype(jnp.int32)
        target[...] = jnp.where(lane == LIST - 1, (every - position + 3) >> 2, packed)


def make_lists(counts, pairs, wanted):
    list_type = jax.ShapeDtypeStruct((1, LIST), jnp.int32)
    return call(
        list_kernel, "lists", [SMEM, VMEM, VMEM], [(VMEM, list_type)] * 3, [],
    )(counts, jnp.transpose(pairs[0], (0, 2, 1)), wanted)


def unpack_slab(block, rows, boxes, base, member_of):
    start = pl.multiple_of(MARGIN + 8 * member_of, 8)

    def one(k, carry):
        for c in range(CHUNKS):
            part = block[pl.ds(k * 16, 16), c * 128 : (c + 1) * 128].astype(F32)
            boxes[pl.ds(base + 2 * k, 2), c, pl.ds(start, 8), :] = part.reshape(2, 8, 128)
        return carry

    lax.fori_loop(0, rows // 16, one, 0, unroll=4)


def fill(refs, boxes, base):
    position = lax.axis_index("grp")
    for k, ref in enumerate(refs):
        unpack_slab(ref, ref.shape[0], boxes, base, (position - k) & 3)


def run_pairs(base, slot, anchors, wanted, listed, boxes, sums, blocks, along_x, inverse, work):
    density, one, two, three, field = work
    first, second = sums
    member = lax.axis_index("orb")
    batches = (listed[0, LIST - 1] + BATCH - 1) // BATCH
    field[...] = jnp.zeros_like(field)

    def fields(k):
        entry = listed[0, k]
        i = entry & 31
        c = (entry >> 5) & 31
        if base:
            other = jnp.maximum(wanted[member, slot + c], 0)
        else:
            other = member * 32 + c
        shifted = MARGIN + anchors[member * 32 + i] - anchors[other]
        return (i, c, shifted, (entry >> 11).astype(F32))

    def part(p, h):
        return (slice(p * EXT, (p + 1) * EXT), slice(h * 128, (h + 1) * 128))

    def quads(a, b, c, d):
        s1, s2, s3, s4 = a + b, a - b, c + d, c - d
        return (s1 + s3, s2 + s4, s1 - s3, s2 - s4)

    def product(b, p):
        i, c, shifted, _ = fields(b * BATCH + p)
        for h in range(2):
            f = [
                boxes[i, 2 * q + h, pl.ds(MARGIN, EXT), :] * boxes[base + c, 2 * q + h, pl.ds(shifted, EXT), :]
                for q in range(4)
            ]
            rows, lanes = part(p, h)
            for q, v in enumerate(quads(*f)):
                density[q, rows, lanes] = v.astype(BF16)

    def terms(b, p):
        i, c, shifted, weight = fields(b * BATCH + p)
        for h in range(2):
            rows, lanes = part(p, h)
            v = [u * weight for u in quads(*(field[q, rows, lanes] for q in range(4)))]
            for q in range(4):
                first[i, 2 * q + h] += v[q] * boxes[base + c, 2 * q + h, pl.ds(shifted, EXT), :]
            for q in range(4):
                second[c, 2 * q + h, pl.ds(shifted, EXT), :] += v[q] * boxes[i, 2 * q + h, pl.ds(MARGIN, EXT), :]

    def step(stage, q):
        if stage == 0:
            one[q] = jnp.dot(density[q], blocks[q], preferred_element_type=F32).astype(BF16)
        elif stage == 1:
            t = jnp.dot(along_x[...], one[q], preferred_element_type=F32)
            two[q] = (t.reshape(BATCH, EXT, 256) * inverse[q][None]).reshape(BATCH * EXT, 256).astype(BF16)
        elif stage == 2:
            three[q] = jnp.dot(along_x[...], two[q], preferred_element_type=F32).astype(BF16)
        else:
            field[q] = lax.dot_general(three[q], blocks[q], (((1,), (1,)), ((), ())), preferred_element_type=F32)

    def batch(b, carry):
        for k in range(8):
            step(k // 4, k % 4)
            terms(jnp.maximum(b - 1, 0), k)
        for k in range(8):
            step(2 + k // 4, k % 4)
            product(b + 1, k)
        return carry

    for p in range(BATCH):
        product(0, p)
    lax.fori_loop(0, batches, batch, 0)
    for p in range(BATCH):
        terms(jnp.maximum(batches - 1, 0), p)


def prepare(boxes, sums):
    first, second = sums

    def margins(k, carry):
        for c in range(CHUNKS):
            boxes[k, c, 0:MARGIN, :] = jnp.zeros((MARGIN, 128), F32)
            boxes[k, c, MARGIN + EXT : PAD, :] = jnp.zeros((MARGIN, 128), F32)
        return carry

    lax.fori_loop(0, boxes.shape[0], margins, 0, unroll=4)

    def blank(k, carry):
        first[pl.ds(k, 1)] = jnp.zeros((1, CHUNKS, EXT, 128), F32)
        return carry

    def blank_second(k, carry):
        second[pl.ds(k, 1), :, MARGIN : MARGIN + EXT, :] = jnp.zeros((1, CHUNKS, EXT, 128), F32)
        return carry

    lax.fori_loop(0, first.shape[0], blank, 0, unroll=2)
    lax.fori_loop(0, second.shape[0], blank_second, 0, unroll=2)


def pack_sums(outs, terms, before=None):
    position = lax.axis_index("grp")
    for step, target in enumerate(outs):
        start = 8 * ((position + step) & 3)

        def one(k, carry):
            for c in range(CHUNKS):
                value = None
                for ref, margin in terms:
                    rows = pl.ds(pl.multiple_of(start + margin, 8), 8)
                    term = ref[pl.ds(2 * k, 2), c, rows, :].reshape(16, 128)
                    value = term if value is None else value + term
                cell = (pl.ds(pl.multiple_of(k * 16, 16), 16), slice(c * 128, (c + 1) * 128))
                if before:
                    value = value + before[step][cell].astype(F32)
                target[cell] = value.astype(BF16)
            return carry

        lax.fori_loop(0, target.shape[0] // 16, one, 0, unroll=4)


def own_kernel(anchors, wanted, listed, *rest):
    own = rest[:4]
    blocks, along_x, inverse = rest[4:7]
    outs, boxes, sums, work = rest[7:11], rest[11], rest[12:14], rest[14:]
    prepare(boxes, sums)
    fill(own, boxes, 0)
    run_pairs(0, 0, anchors, wanted, listed, boxes, sums, blocks, along_x, inverse, work)
    pack_sums(outs, ((sums[0], 0), (sums[1], MARGIN)))


def far_kernel(slot, anchors, wanted, listed, *rest):
    before, own, far = rest[:4], rest[4:8], rest[8:12]
    blocks, along_x, inverse = rest[12:15]
    own_outs, far_outs, boxes, sums, work = rest[15:19], rest[19:23], rest[23], rest[24:26], rest[26:]
    prepare(boxes, sums)
    fill(own, boxes, 0)
    fill(far, boxes, 32)
    run_pairs(32, slot, anchors, wanted, listed, boxes, sums, blocks, along_x, inverse, work)
    pack_sums(far_outs, ((sums[1], MARGIN),))
    pack_sums(own_outs, ((sums[0], 0),), before)


def scratch(total):
    stage = pltpu.VMEM((4, BATCH * EXT, 256), BF16)
    return [
        pltpu.VMEM((total, CHUNKS, PAD, 128), F32),
        pltpu.VMEM((32, CHUNKS, EXT, 128), F32),
        pltpu.VMEM((32 if total == 32 else total - 32, CHUNKS, PAD, 128), F32),
        stage, stage, stage, stage,
        pltpu.VMEM((4, BATCH * EXT, 256), F32),
    ]


def finish_kernel(wanted, p0, p1, p2, p3, returned, out, matrix, total):
    member = lax.axis_index("orb")
    for c in range(CHUNKS):
        source = source_of(lax.broadcasted_iota(jnp.int32, (PLANE, 128), 0))
        column = lax.broadcasted_iota(jnp.int32, (PLANE, 128), 1) + c * 128
        matrix[:, c * 128 : (c + 1) * 128] = (column == source).astype(F32).astype(BF16)
    total[...] = (p0[...].astype(F32) + p1[...].astype(F32)) + (p2[...].astype(F32) + p3[...].astype(F32))
    for r in range(0, 32, 2):
        both = returned[r * 8 : r * 8 + 16, :].astype(F32)
        for u in range(2):
            asked = wanted[r + u, member]
            row = pl.multiple_of(jnp.clip(asked - member * 32, 0, 31) * 8, 8)

            @pl.when(asked >= 0)
            def _():
                total[pl.ds(row, 8), :] += both[u * 8 : (u + 1) * 8]

    value = total[...]
    high = value.astype(BF16)
    low = (value - high.astype(F32)).astype(BF16)
    out[...] = jnp.dot(high, matrix[...], preferred_element_type=F32) + jnp.dot(
        low, matrix[...], preferred_element_type=F32
    )


SMEM = pl.BlockSpec(memory_space=pltpu.SMEM)
VMEM = pl.BlockSpec(memory_space=pltpu.VMEM)


SLAB = jax.ShapeDtypeStruct((256, PLANE), BF16)
HALF_SLAB = jax.ShapeDtypeStruct((128, PLANE), BF16)
OWN_PARTS = [(VMEM, SLAB)] * 4
FAR_PARTS = [(VMEM, HALF_SLAB)] * 4


def call(kernel, name, ins, outs, scratch, limit=24):
    return pl.pallas_call(
        kernel,
        name=name,
        in_specs=ins,
        out_specs=[spec for spec, _ in outs],
        out_shape=[shape for _, shape in outs],
        scratch_shapes=scratch,
        compiler_params=pltpu.CompilerParams(vmem_limit_bytes=limit << 20),
    )


def shift(block, step):
    return lax.ppermute(block, "grp", [(m, (m + step) % 4) for m in range(4)])


def gather(slab):
    return (slab, *(shift(slab, step) for step in (1, 2, 3)))


def scatter(parts):
    return (parts[0], *(shift(parts[step], step) for step in (1, 2, 3)))


def shards(orbitals, anchors, wanted, pairs, counts):
    blocks, along_x, inverse = (jnp.asarray(t) for t in tables())
    wanted = wanted.reshape(32, 32)
    slab, outgoing = call(
        order_kernel, "order", [SMEM, VMEM], [(VMEM, SLAB)] * 2,
        [pltpu.VMEM((PLANE, PLANE), BF16), pltpu.VMEM((256, PLANE), F32)],
    )(wanted, orbitals.reshape(256, PLANE))
    with jax.named_scope("own_gather"):
        own = gather(slab)
    with jax.named_scope("partners"):
        incoming = lax.all_to_all(outgoing, "orb", split_axis=0, concat_axis=0, tiled=True)
    own_list, *far_lists = make_lists(counts, pairs, wanted)
    with jax.named_scope("low_gather"):
        low = gather(incoming[:128])
    with jax.named_scope("high_gather"):
        high = gather(incoming[128:])
    tables_in = (blocks, along_x, inverse)
    with jax.named_scope("own_pairs"):
        sums = call(own_kernel, "own", [SMEM] * 3 + [VMEM] * 7, OWN_PARTS, scratch(32), 30)(
            anchors, wanted, own_list, *own, *tables_in
        )
    returning = []
    for k, (name, far) in enumerate((("low", low), ("high", high))):
        with jax.named_scope(name + "_pairs"):
            kernel = functools.partial(far_kernel, 16 * k)
            parts = call(kernel, name, [SMEM] * 3 + [VMEM] * 15, OWN_PARTS + FAR_PARTS, scratch(48), 36)(
                anchors, wanted, far_lists[k], *sums, *own, *far, *tables_in
            )
        sums = parts[:4]
        with jax.named_scope(name + "_scatter"):
            returning.append(scatter(parts[4:]))
    with jax.named_scope("own_scatter"):
        own_got = scatter(sums)
    far_sum = jnp.concatenate(
        [sum(part.astype(F32) for part in got).astype(BF16) for got in returning], axis=0
    )
    with jax.named_scope("owners"):
        returned = lax.all_to_all(far_sum, "orb", split_axis=0, concat_axis=0, tiled=True)
    (result,) = call(
        finish_kernel, "finish", [SMEM] + [VMEM] * 5,
        [(VMEM, jax.ShapeDtypeStruct((256, PLANE), F32))],
        [pltpu.VMEM((PLANE, PLANE), BF16), pltpu.VMEM((256, PLANE), F32)],
    )(wanted, *own_got, returned)
    return result.reshape(32, 8, PLANE)


def solution(mesh):
    return jax.shard_map(
        shards,
        mesh=mesh,
        in_specs=(P("orb", "grp", None), P(), P(), P("orb", None, None, None), P("orb", None)),
        out_specs=P("orb", "grp", None),
        check_vma=False,
    )
```
